128 devices in a mesh: outer: 16 (over x, y), inner: 8 (over z, core).
Axes of the slice: x: 4, y: 4, z: 4, core: 2. Of those that a mesh axis runs over, the one named last changes fastest.
Arguments:
- query_proj: bfloat16 [196608, 2048], P(('outer', 'inner')), may hold values from -6 to 6
- key_proj: bfloat16 [196608, 2048], P(('outer', 'inner')), may hold values from -6 to 6
- value_proj: bfloat16 [196608, 2048], P(('outer', 'inner')), may hold values from -6 to 6
- norm_gain: float32 [2048], replicated, may hold values from 0.25 to 1.75
Outputs:
- attended: bfloat16 [196608, 2048], P(('outer', 'inner'))
The draws below stay inside these ranges and needn't reach their ends.
All inputs are finite; a program needn't handle non-finite values.
Results may differ from the reference program's by a relative error of at most 0.0049.
Values sent between devices are 32-bit elements; how exact they have to be, the bound alone decides.
No kernel may reach another device: no remote copies, remote signals or barrier semaphores. Data moves between devices by JAX's collectives and lax.ppermute only.
A program may use at most 192 MiB of HBM per device.

```python
import jax
import jax.numpy as jnp
from jax import lax

H = 16
DK = 128
SPAN = 256
SEQ = 196608
HD = 2048


def block_levels(key, shape, shards, low, top_value):
    level = 1.0
    for position, blocks in shards:
        heights = jax.random.uniform(jax.random.fold_in(jax.random.fold_in(key, 6), position), (blocks,), jnp.float32, low / len(shards), top_value / len(shards))
        level = level * jnp.repeat(jnp.exp(heights), shape[position] // blocks).reshape((-1,) + (1,) * (len(shape) - 1 - position))
    return level


def noise(stream_key, shape, scale, bound, shards=(), dtype=jnp.bfloat16):
    array = scale * jax.random.normal(stream_key, shape, jnp.float32)
    if shards:
        array = array * block_levels(stream_key, shape, shards, -0.22, 0.18)
    return jnp.clip(array, -bound, bound).astype(dtype)


def setup_inputs(seed: int = 0) -> dict:
    keys = jax.random.split(jax.random.key(seed), 5)
    return {
        "query_proj": noise(keys[0], (SEQ, HD), 1.0, 6.0, ((0, 128),)),
        "key_proj": noise(keys[1], (SEQ, HD), 1.0, 6.0, ((0, 128),)),
        "value_proj": noise(keys[2], (SEQ, HD), 1.0, 6.0, ((0, 128),)),
        "norm_gain": jnp.clip(1.0 + 0.15 * jax.random.normal(keys[3], (HD,), jnp.float32), 0.25, 1.75),
    }


def reference(query_proj, key_proj, value_proj, norm_gain):
    count = SEQ // SPAN
    shape = (count, SPAN, H, DK)
    queries = query_proj.reshape(shape)
    keys_all = key_proj.reshape(shape)
    values_all = value_proj.reshape(shape)
    rows = jnp.arange(SPAN)
    causal = rows[:, None] >= rows[None, :]
    gain = norm_gain.reshape(H, DK)

    def step(state, blocks):
        query_block, key_block, value_block = blocks
        qfloat = query_block.astype(jnp.float32)
        kfloat = key_block.astype(jnp.float32)
        vfloat = value_block.astype(jnp.float32)
        rounded = lax.optimization_barrier(state.astype(jnp.bfloat16)).astype(jnp.float32)
        carried = jnp.einsum('chd,hde->che', qfloat, rounded)
        scores = jnp.einsum('chd,shd->hcs', qfloat, kfloat)
        scores = jnp.where(causal[None], scores, 0.0)
        scores = lax.optimization_barrier(scores.astype(jnp.bfloat16)).astype(jnp.float32)
        local = jnp.einsum('hcs,she->che', scores, vfloat)
        raw = carried + local
        state = state + jnp.einsum('chd,che->hde', kfloat, vfloat)
        meansq = lax.optimization_barrier(jnp.mean(raw * raw, axis=-1, keepdims=True))
        normed = raw * lax.rsqrt(meansq + 1e-06) * gain
        return (state, normed.astype(jnp.bfloat16).reshape(SPAN, H * DK))
    start = jnp.zeros((H, DK, DK), jnp.float32)
    _, outputs = lax.scan(step, start, (queries, keys_all, values_all))
    return outputs.reshape(SEQ, H * DK)
```

```python
import functools

import jax
import jax.numpy as jnp
from jax import lax
from jax.experimental import pallas as pl
from jax.experimental.pallas import tpu as pltpu
from jax.sharding import Mesh
from jax.sharding import PartitionSpec as P

H = 16
DK = 128
SPAN = 256
HALF = H // 2
CHIPS = ("x", "y", "z")
ALL = ("x", "y", "z", "c")
PAIR = 2 * DK
F32 = jnp.float32
BF16 = jnp.bfloat16


def in_hbm(array):
    return pltpu.with_memory_space_constraint(array, pltpu.HBM)


def state_kernel(half_ref, k_ref, v_ref, o_ref):
    for h in range(2):
        cols = slice(h * DK, (h + 1) * DK)
        o_ref[cols, :] = lax.dot_general(
            k_ref[:, cols], v_ref[:, cols], (((0,), (0,)), ((), ())), preferred_element_type=F32
        )


def half_states(half, keys, values):
    tokens = keys.shape[0]
    steps = HALF // 2
    block = pl.BlockSpec((tokens, PAIR), lambda i, half: (0, half[0] * steps + i))
    return pl.pallas_call(
        state_kernel,
        out_shape=jax.ShapeDtypeStruct((HALF * DK, DK), F32),
        grid_spec=pltpu.PrefetchScalarGridSpec(
            num_scalar_prefetch=1,
            grid=(steps,),
            in_specs=[block, block],
            out_specs=pl.BlockSpec((PAIR, DK), lambda i, half: (i, 0)),
        ),
        compiler_params=pltpu.CompilerParams(vmem_limit_bytes=16 * 2**20),
        cost_estimate=pl.CostEstimate(
            flops=2 * tokens * HALF * DK * DK, bytes_accessed=4 * tokens * HALF * DK, transcendentals=0
        ),
        name="half_states",
    )(half, in_hbm(keys), in_hbm(values))


def local_kernel(q_ref, k_ref, v_ref, o_ref):
    count = q_ref.shape[0] // SPAN
    rows = lax.broadcasted_iota(jnp.int32, (SPAN, SPAN), 0)
    cols = lax.broadcasted_iota(jnp.int32, (SPAN, SPAN), 1)
    causal = rows >= cols
    for h in range(2):
        lanes = slice(h * DK, (h + 1) * DK)
        running = None
        for n in range(count):
            span = slice(n * SPAN, (n + 1) * SPAN)
            q, k, v = q_ref[span, lanes], k_ref[span, lanes], v_ref[span, lanes]
            scores = lax.dot_general(q, k, (((1,), (1,)), ((), ())), preferred_element_type=F32)
            scores = jnp.where(causal, scores, 0.0).astype(BF16)
            out = jnp.dot(scores, v, preferred_element_type=F32)
            if n:
                out += jnp.dot(q, running.astype(BF16), preferred_element_type=F32)
            if n < count - 1:
                state = lax.dot_general(k, v, (((0,), (0,)), ((), ())), preferred_element_type=F32)
                running = state if running is None else running + state
            o_ref[span, lanes] = out


def local_part(queries, keys, values):
    tokens, width = queries.shape
    block = pl.BlockSpec((tokens, PAIR), lambda i: (0, i))
    return pl.pallas_call(
        local_kernel,
        out_shape=pltpu.HBM((tokens, width), F32),
        grid=(width // PAIR,),
        in_specs=[block, block, block],
        out_specs=block,
        compiler_params=pltpu.CompilerParams(vmem_limit_bytes=32 * 2**20),
        cost_estimate=pl.CostEstimate(
            flops=6 * tokens * width * SPAN, bytes_accessed=10 * tokens * width, transcendentals=0
        ),
        name="local_part",
    )(in_hbm(queries), in_hbm(keys), in_hbm(values))


def scan_kernel(x_ref, o_ref):
    total = jnp.zeros(x_ref.shape[1:], F32)
    for j in range(x_ref.shape[0]):
        o_ref[j] = total
        total += x_ref[j]


def earlier_sums(x):
    return pl.pallas_call(
        scan_kernel,
        out_shape=jax.ShapeDtypeStruct(x.shape, x.dtype),
        compiler_params=pltpu.CompilerParams(vmem_limit_bytes=4 * 2**20),
        name="earlier_sums",
    )(x)


def core_kernel(core_ref, chip_ref, mine_ref, theirs_ref, own_ref, partner_ref):
    first = chip_ref[...]

    @pl.when(core_ref[0] == 0)
    def _():
        own_ref[...] = first
        partner_ref[...] = first + mine_ref[...]

    @pl.when(core_ref[0] == 1)
    def _():
        own_ref[...] = first + theirs_ref[...]
        partner_ref[...] = first


def core_prefixes(core, before_chip, mine, theirs):
    whole = pl.BlockSpec(memory_space=pltpu.VMEM)
    return pl.pallas_call(
        core_kernel,
        out_shape=[jax.ShapeDtypeStruct(before_chip.shape, F32)] * 2,
        in_specs=[pl.BlockSpec(memory_space=pltpu.SMEM), whole, whole, whole],
        out_specs=[whole, whole],
        compiler_params=pltpu.CompilerParams(vmem_limit_bytes=8 * 2**20),
        name="core_prefixes",
    )(core, before_chip, mine, theirs)


def output_kernel(half_ref, q_ref, local_ref, prefix_ref, gain_ref, *rest):
    o_ref = rest[-1]
    ones = jnp.full((DK, DK), 1.0 / DK, BF16)
    for h in range(2):
        lanes = slice(h * DK, (h + 1) * DK)
        prefix = prefix_ref[lanes, :].astype(BF16)
        gain = gain_ref[:, lanes]
        for n in range(q_ref.shape[0] // SPAN):
            span = slice(n * SPAN, (n + 1) * SPAN)
            raw = local_ref[span, lanes] + jnp.dot(q_ref[span, lanes], prefix, preferred_element_type=F32)
            meansq = jnp.dot((raw * raw).astype(BF16), ones, preferred_element_type=F32)
            o_ref[span, lanes] = (raw * lax.rsqrt(meansq + 1e-06) * gain).astype(BF16)


def half_output(half, queries, local, prefix, gain, partial):
    tokens, width = queries.shape
    steps = HALF // 2
    block = pl.BlockSpec((tokens, PAIR), lambda i, half: (0, half[0] * steps + i))
    in_specs = [
        block,
        block,
        pl.BlockSpec((PAIR, DK), lambda i, half: (i, 0)),
        pl.BlockSpec((1, PAIR), lambda i, half: (0, half[0] * steps + i)),
    ]
    args = [half, in_hbm(queries), in_hbm(local), prefix, gain]
    alias = {}
    if partial is not None:
        in_specs.append(pl.BlockSpec(memory_space=pl.ANY))
        args.append(partial)
        alias = {5: 0}
    return pl.pallas_call(
        output_kernel,
        out_shape=jax.ShapeDtypeStruct((tokens, width), BF16),
        grid_spec=pltpu.PrefetchScalarGridSpec(
            num_scalar_prefetch=1, grid=(steps,), in_specs=in_specs, out_specs=block
        ),
        input_output_aliases=alias,
        compiler_params=pltpu.CompilerParams(vmem_limit_bytes=24 * 2**20),
        cost_estimate=pl.CostEstimate(
            flops=4 * tokens * HALF * DK * DK, bytes_accessed=8 * tokens * HALF * DK, transcendentals=0
        ),
        name="half_output",
    )(*args)


def shards(queries, keys, values, norm_gain):
    core = lax.axis_index("c")
    own = core.astype(jnp.int32).reshape(1)
    other = 1 - own
    swap = functools.partial(lax.ppermute, axis_name="c", perm=[(0, 1), (1, 0)])
    theirs = swap(half_states(other, keys, values))
    mine = half_states(own, keys, values)
    chip = mine + theirs
    chips = lax.axis_size("x") * lax.axis_size("y") * lax.axis_size("z")
    pieces = lax.all_to_all(chip, CHIPS, 0, 0, tiled=True)
    local = local_part(queries, keys, values)
    sums = earlier_sums(pieces.reshape(chips, -1, DK)).reshape(pieces.shape)
    before_chip = lax.all_to_all(sums, CHIPS, 0, 0, tiled=True)
    prefix_own, prefix_partner = core_prefixes(own, before_chip, mine, theirs)
    prefix_other = swap(prefix_partner)
    gain = norm_gain.reshape(1, -1)
    out = half_output(own, queries, local, prefix_own, gain, None)
    return half_output(other, queries, local, prefix_other, gain, out)


def solution(mesh):
    finer = Mesh(mesh.devices.reshape(4, 4, mesh.shape["inner"] // 2, 2), ALL)
    return jax.shard_map(
        shards, mesh=finer, in_specs=(P(ALL, None),) * 3 + (P(),), out_specs=P(ALL, None), check_vma=False
    )
```

```python
import functools

import jax
import jax.numpy as jnp
from jax import lax
from jax.experimental import pallas as pl
from jax.experimental.pallas import tpu as pltpu
from jax.sharding import Mesh
from jax.sharding import PartitionSpec as P

H = 16
DK = 128
SPAN = 256
HALF = H // 2
CHIPS = ("x", "y", "z")
ALL = ("x", "y", "z", "c")
PAIR = 2 * DK
CHUNKS = HALF // 2
WIDTH = HALF * DK
MIB = 2**20
F32 = jnp.float32
BF16 = jnp.bfloat16
SMEM = pl.BlockSpec(memory_space=pltpu.SMEM)
VMEM = pl.BlockSpec(memory_space=pltpu.VMEM)
IN_HBM = pl.BlockSpec(memory_space=pltpu.HBM)


def in_hbm(array):
    return pltpu.with_memory_space_constraint(array, pltpu.HBM)


def kernel_call(kernel, out_shape, in_specs, out_specs, scratch, vmem_mib, flops, moved, alias=None):
    return pl.pallas_call(
        kernel,
        out_shape=out_shape,
        in_specs=in_specs,
        out_specs=out_specs,
        scratch_shapes=scratch,
        input_output_aliases=alias or {},
        compiler_params=pltpu.CompilerParams(vmem_limit_bytes=vmem_mib * MIB),
        cost_estimate=pl.CostEstimate(flops=flops, bytes_accessed=moved, transcendentals=0),
    )


def lanes_of(base, i):
    return pl.ds(pl.multiple_of(base + i * PAIR, PAIR), PAIR)


def two_blocks(first, second):
    top = jnp.concatenate([first, jnp.zeros(second.shape, second.dtype)], axis=1)
    bottom = jnp.concatenate([jnp.zeros(first.shape, first.dtype), second], axis=1)
    return jnp.concatenate([top, bottom], axis=0)


def score(a, b):
    return lax.dot_general(a, b, (((1,), (1,)), ((), ())), preferred_element_type=F32)


def tokens_dot(a, b):
    return lax.dot_general(a, b, (((0,), (0,)), ((), ())), preferred_element_type=F32)


AHEAD = 2


def half_cols(half):
    return pl.ds(pl.multiple_of(half * WIDTH, WIDTH), WIDTH)


def block_copies(k_hbm, v_hbm, k_buf, v_buf, sems, cols, n, slot, sem):
    rows = pl.ds(n * SPAN, SPAN)
    return (
        pltpu.make_async_copy(k_hbm.at[rows, cols], k_buf.at[slot], sems.at[0, sem]),
        pltpu.make_async_copy(v_hbm.at[rows, cols], v_buf.at[slot], sems.at[1, sem]),
    )


def add_state(n, count, k, v, o_ref, earlier_buf=None):
    for i in range(CHUNKS):
        pair = tokens_dot(k[:, i * PAIR : (i + 1) * PAIR], v[:, i * PAIR : (i + 1) * PAIR])
        for h in range(2):
            rows = slice(i * PAIR + h * DK, i * PAIR + (h + 1) * DK)
            state = pair[h * DK : (h + 1) * DK, h * DK : (h + 1) * DK]
            if n:
                state += o_ref[rows, :]
            o_ref[rows, :] = state
            if earlier_buf is not None and n < count - 1:
                earlier_buf[n, rows, :] = state.astype(BF16)


def states_of(blocks, copies, o_ref, earlier_hbm=None, earlier_buf=None, sems=None):
    count = len(blocks)
    outs = []
    for n, (k_buf, v_buf, slot) in enumerate(blocks):
        if n % 2 == 0:
            for copy in copies[n] + copies[n + 1]:
                copy.wait()
        add_state(n, count, k_buf[slot], v_buf[slot], o_ref, earlier_buf)
        if earlier_buf is not None and n < count - 1:
            outs.append(pltpu.make_async_copy(earlier_buf.at[n], earlier_hbm.at[n], sems.at[2, n]))
            outs[-1].start()
    for copy in outs:
        copy.wait()


def first_states_kernel(half_ref, k_hbm, v_hbm, o_ref, earlier_hbm, k_next, v_next, k_buf, v_buf, earlier_buf, sems):
    count = k_buf.shape[0]
    cols, next_cols = half_cols(half_ref[0]), half_cols(1 - half_ref[0])
    copies = [block_copies(k_hbm, v_hbm, k_buf, v_buf, sems, cols, n, n, n) for n in range(count)]
    ahead = [
        block_copies(k_hbm, v_hbm, k_next, v_next, sems, next_cols, n, n, count + n) for n in range(AHEAD)
    ]
    for pair in copies + ahead:
        for copy in pair:
            copy.start()
    states_of([(k_buf, v_buf, n) for n in range(count)], copies, o_ref, earlier_hbm, earlier_buf, sems)
    for pair in ahead:
        for copy in pair:
            copy.wait()


def second_states_kernel(half_ref, k_hbm, v_hbm, k_first, v_first, o_ref, k_buf, v_buf, sems):
    rest = k_buf.shape[0]
    cols = half_cols(half_ref[0])
    copies = [()] * AHEAD + [
        block_copies(k_hbm, v_hbm, k_buf, v_buf, sems, cols, AHEAD + n, n, n) for n in range(rest)
    ]
    for pair in copies:
        for copy in pair:
            copy.start()
    blocks = [(k_first, v_first, n) for n in range(AHEAD)] + [(k_buf, v_buf, n) for n in range(rest)]
    states_of(blocks, copies, o_ref)


def half_states(half, keys, values, ahead=None):
    tokens = keys.shape[0]
    count = tokens // SPAN
    first = ahead is None
    buf = pltpu.VMEM((count if first else count - AHEAD, SPAN, WIDTH), BF16)
    out_shape, out_specs = [jax.ShapeDtypeStruct((WIDTH, DK), F32)], [VMEM]
    scratch = [buf, buf, pltpu.SemaphoreType.DMA((3, count + AHEAD))]
    if first:
        out_shape += [pltpu.HBM((count - 1, WIDTH, DK), BF16)] + [pltpu.VMEM((AHEAD, SPAN, WIDTH), BF16)] * 2
        out_specs += [IN_HBM, VMEM, VMEM]
        scratch.insert(2, pltpu.VMEM((count - 1, WIDTH, DK), BF16))
    return kernel_call(
        first_states_kernel if first else second_states_kernel,
        out_shape,
        [SMEM, IN_HBM, IN_HBM] + [VMEM] * (0 if first else 2),
        out_specs,
        scratch,
        16,
        2 * tokens * HALF * DK * DK,
        4 * tokens * WIDTH,
    )(half, in_hbm(keys), in_hbm(values), *(ahead or ()))


def local_kernel(with_states, half_ref, q_hbm, k_hbm, v_hbm, *rest):
    if with_states:
        o_hbm, earlier_hbm, q_buf, k_buf, v_buf, o_buf, sems, sum_buf, earlier_buf = rest
    else:
        o_hbm, q_buf, k_buf, v_buf, o_buf, sems = rest
    base = half_ref[0] * WIDTH
    count = q_buf.shape[1] // SPAN
    rows = lax.broadcasted_iota(jnp.int32, (DK, PAIR), 0)
    cols = lax.broadcasted_iota(jnp.int32, (DK, PAIR), 1) % DK
    causal = rows >= cols

    def copies(i):
        lanes = lanes_of(base, i)
        return [
            pltpu.make_async_copy(hbm.at[:, lanes], buf.at[i], sems.at[j, i])
            for j, (hbm, buf) in enumerate(((q_hbm, q_buf), (k_hbm, k_buf), (v_hbm, v_buf)))
        ]

    def out_copies(i):
        lanes = lanes_of(0, i)
        outs = [pltpu.make_async_copy(o_buf.at[i], o_hbm.at[:, lanes], sems.at[3, i])]
        if with_states:
            outs.append(pltpu.make_async_copy(earlier_buf.at[i], earlier_hbm.at[:, lanes, :], sems.at[4, i]))
        return outs

    for i in range(CHUNKS):
        for copy in copies(i):
            copy.start()

    def chunk(i, carry):
        for copy in copies(i):
            copy.wait()

        def pairs_of(buf, n):
            rows = [buf[i, n * SPAN + j * DK : n * SPAN + (j + 1) * DK, :] for j in range(2)]
            return [two_blocks(r[:, :DK], r[:, DK:]) for r in rows]

        def scores_of(n):
            start = n * SPAN
            first_keys, second_keys = pairs_of(k_buf, n)
            top = score(q_buf[i, start : start + DK, :], first_keys)
            bottom = score(q_buf[i, start + DK : start + SPAN, :], first_keys)
            corner = score(q_buf[i, start + DK : start + SPAN, :], second_keys)
            return (
                jnp.where(causal, top, 0.0).astype(BF16),
                bottom.astype(BF16),
                jnp.where(causal, corner, 0.0).astype(BF16),
            )

        ready = scores_of(0)
        for n in range(count):
            top, bottom, corner = ready
            if n < count - 1:
                ready = scores_of(n + 1)
            first_values, second_values = pairs_of(v_buf, n)
            start = n * SPAN
            out_top = jnp.dot(top, first_values, preferred_element_type=F32)
            out_bottom = jnp.dot(bottom, first_values, preferred_element_type=F32)
            out_bottom += jnp.dot(corner, second_values, preferred_element_type=F32)
            o_buf[i, start : start + DK, :] = out_top.astype(BF16)
            o_buf[i, start + DK : start + SPAN, :] = out_bottom.astype(BF16)
            if with_states and n < count - 1:
                pair = tokens_dot(k_buf[i, start : start + SPAN, :], v_buf[i, start : start + SPAN, :])
                for h in range(2):
                    rows = slice(h * DK, (h + 1) * DK)
                    state = pair[rows, rows]
                    if n:
                        state += sum_buf[rows, :]
                    sum_buf[rows, :] = state
                    earlier_buf[i, n, rows, :] = state.astype(BF16)
        for copy in out_copies(i):
            copy.start()
        return carry

    lax.fori_loop(0, CHUNKS, chunk, 0)
    for i in range(CHUNKS):
        for copy in out_copies(i):
            copy.wait()


def local_part(half, queries, keys, values, with_states):
    tokens = queries.shape[0]
    earlier = tokens // SPAN - 1
    buf = pltpu.VMEM((CHUNKS, tokens, PAIR), BF16)
    out_shape, out_specs = [pltpu.HBM((tokens, WIDTH), BF16)], [IN_HBM]
    scratch = [buf, buf, buf, buf, pltpu.SemaphoreType.DMA((5, CHUNKS))]
    if with_states:
        out_shape.append(pltpu.HBM((earlier, WIDTH, DK), BF16))
        out_specs.append(IN_HBM)
        scratch += [pltpu.VMEM((PAIR, DK), F32), pltpu.VMEM((CHUNKS, earlier, PAIR, DK), BF16)]
    return kernel_call(
        functools.partial(local_kernel, with_states),
        out_shape,
        [SMEM, IN_HBM, IN_HBM, IN_HBM],
        out_specs,
        scratch,
        18,
        6 * tokens * WIDTH * SPAN,
        8 * tokens * WIDTH,
    )(half, in_hbm(queries), in_hbm(keys), in_hbm(values))


def scan_kernel(x_ref, o_ref):
    total = jnp.zeros(x_ref.shape[1:], F32)
    for j in range(x_ref.shape[0]):
        o_ref[j] = total
        total += x_ref[j]


def add_kernel(a_ref, b_ref, o_ref):
    o_ref[...] = a_ref[...] + b_ref[...]


def small_call(kernel, *args):
    shape, size = args[0].shape, args[0].size
    return kernel_call(kernel, pltpu.VMEM(shape, F32), [VMEM] * len(args), VMEM, [], 4, size, 12 * size)(*args)


def core_kernel(core_ref, chip_ref, mine_ref, theirs_ref, own_ref, partner_ref):
    first = chip_ref[...]

    @pl.when(core_ref[0] == 0)
    def _():
        own_ref[...] = first
        partner_ref[...] = first + mine_ref[...]

    @pl.when(core_ref[0] == 1)
    def _():
        own_ref[...] = first + theirs_ref[...]
        partner_ref[...] = first


def core_prefixes(core, before_chip, mine, theirs):
    size = before_chip.size
    return kernel_call(
        core_kernel,
        [jax.ShapeDtypeStruct(before_chip.shape, F32)] * 2,
        [SMEM, VMEM, VMEM, VMEM],
        [VMEM, VMEM],
        [],
        8,
        size,
        20 * size,
    )(core, before_chip, mine, theirs)


def output_kernel(half_ref, q_hbm, local_hbm, earlier_hbm, prefix_ref, gain_ref, *rest):
    o_hbm, q_buf, local_buf, earlier_buf, o_buf, sems = rest[-6:]
    base = half_ref[0] * WIDTH
    tokens = q_buf.shape[1]

    def copies(i):
        return (
            pltpu.make_async_copy(q_hbm.at[:, lanes_of(base, i)], q_buf.at[i], sems.at[0, i]),
            pltpu.make_async_copy(local_hbm.at[:, lanes_of(0, i)], local_buf.at[i], sems.at[1, i]),
            pltpu.make_async_copy(earlier_hbm.at[:, lanes_of(0, i), :], earlier_buf.at[i], sems.at[3, i]),
        )

    def out_copy(i):
        return pltpu.make_async_copy(o_buf.at[i], o_hbm.at[:, lanes_of(base, i)], sems.at[2, i])

    for i in range(CHUNKS):
        for copy in copies(i):
            copy.start()

    def chunk(i, carry):
        for copy in copies(i):
            copy.wait()
        prefix = prefix_ref[pl.ds(pl.multiple_of(i * PAIR, PAIR), PAIR), :]
        gain = gain_ref[:, lanes_of(base, i)] * DK**0.5
        spans = [slice(n * SPAN, (n + 1) * SPAN) for n in range(tokens // SPAN)]
        for n, span in enumerate(spans):
            carried = prefix + earlier_buf[i, n - 1].astype(F32) if n else prefix
            carried = carried.astype(BF16)
            carried = two_blocks(carried[:DK], carried[DK:])
            for part in (slice(span.start, span.start + DK), slice(span.start + DK, span.stop)):
                raw = local_buf[i, part, :] + jnp.dot(q_buf[i, part, :], carried, preferred_element_type=F32)
                for h in range(2):
                    lanes = slice(h * DK, (h + 1) * DK)
                    head = raw[:, lanes]
                    squares = jnp.sum(head * head, axis=-1, keepdims=True)
                    o_buf[i, part, lanes] = (head * lax.rsqrt(squares + DK * 1e-06) * gain[:, lanes]).astype(BF16)
        out_copy(i).start()
        return carry

    lax.fori_loop(0, CHUNKS, chunk, 0)
    for i in range(CHUNKS):
        out_copy(i).wait()


def half_output(half, queries, local, earlier, prefix, gain, partial):
    tokens, width = queries.shape
    in_specs = [SMEM, IN_HBM, IN_HBM, IN_HBM, VMEM, VMEM]
    args = [half, in_hbm(queries), in_hbm(local), in_hbm(earlier), prefix, gain]
    alias = {}
    if partial is not None:
        in_specs.append(IN_HBM)
        args.append(partial)
        alias = {6: 0}
    buf = pltpu.VMEM((CHUNKS, tokens, PAIR), BF16)
    return kernel_call(
        output_kernel,
        jax.ShapeDtypeStruct((tokens, width), BF16),
        in_specs,
        IN_HBM,
        [
            buf,
            buf,
            pltpu.VMEM((CHUNKS, earlier.shape[0], PAIR, DK), BF16),
            buf,
            pltpu.SemaphoreType.DMA((4, CHUNKS)),
        ],
        18,
        4 * tokens * WIDTH * DK,
        8 * tokens * WIDTH,
        alias,
    )(*args)


def shards(queries, keys, values, norm_gain):
    own = lax.axis_index("c").astype(jnp.int32).reshape(1)
    other = 1 - own
    chips = lax.axis_size("x") * lax.axis_size("y") * lax.axis_size("z")
    swap = functools.partial(lax.ppermute, axis_name="c", perm=[(0, 1), (1, 0)])
    others, earlier_other, *ahead = half_states(other, keys, values)
    theirs = swap(others)
    (mine,) = half_states(own, keys, values, ahead)
    chip = small_call(add_kernel, mine, theirs)
    pieces = lax.all_to_all(chip, CHIPS, 0, 0, tiled=True)
    (local_other,) = local_part(other, queries, keys, values, False)
    sums = small_call(scan_kernel, pieces.reshape(chips, -1, DK)).reshape(pieces.shape)
    before_chip = lax.all_to_all(sums, CHIPS, 0, 0, tiled=True)
    local_own, earlier_own = local_part(own, queries, keys, values, True)
    prefix_own, prefix_partner = core_prefixes(own, before_chip, mine, theirs)
    prefix_other = swap(prefix_partner)
    gain = norm_gain.reshape(1, -1)
    out = half_output(own, queries, local_own, earlier_own, prefix_own, gain, None)
    return half_output(other, queries, local_other, earlier_other, prefix_other, gain, out)


def solution(mesh):
    finer = Mesh(mesh.devices.reshape(4, 4, mesh.shape["inner"] // 2, 2), ALL)
    return jax.shard_map(
        shards, mesh=finer, in_specs=(P(ALL, None),) * 3 + (P(),), out_specs=P(ALL, None), check_vma=False
    )
```
